32 devices in a mesh: lon: 8 (over z, y), lat: 2 (over core), mem: 2 (over x).
Axes of the slice: x: 2, y: 2, z: 4, core: 2. Of those that a mesh axis runs over, the one named last changes fastest.
Arguments:
- inputs: bfloat16 [2, 48, 896, 512], P('mem', 'lat', 'lon'), may hold values from -6 to 6
- cotangent: bfloat16 [2, 48, 896, 512], P('mem', 'lat', 'lon'), may hold values from -6 to 6
- dw_kernel: bfloat16 [2, 9, 512], replicated, may hold values from -4 to 4
- pw_weight: bfloat16 [2, 512, 512], replicated, may hold values from -0.25 to 0.25
Outputs:
- input_grad: bfloat16 [2, 48, 896, 512], P('mem', 'lat', 'lon')
- kernel_grad: float32 [2, 9, 512], P(None, None, 'mem')
- weight_grad: float32 [2, 512, 512], P(None, None, 'mem')
The draws below stay inside these ranges and needn't reach their ends.
All inputs are finite; a program needn't handle non-finite values.
Results may differ from the reference program's by a relative error of at most 0.015.
Values may be sent and summed in bfloat16 or wider, within the bound.
A program may use at most 128 MiB of HBM per device.

```python
import math
import jax
import jax.numpy as jnp
from jax import lax

C = 512
KERNEL_SPACING = 4
TAPS = 9
LAYERS = 2
MEMBERS = 2
LAT = 48
LON = 896
SAMPLES = 86016


def draw_dw_kernel(key, part):
    key_scale, key_base = jax.random.split(jax.random.fold_in(key, 17))
    channel_scale = jnp.exp(jax.random.uniform(key_scale, (LAYERS, 1, C), jnp.float32, math.log(0.3), math.log(3.0)))
    base = jnp.clip(jax.random.normal(key_base, (LAYERS, TAPS, C), jnp.float32), -4.0, 4.0)
    return jnp.clip(base * channel_scale / 3.0, -4.0, 4.0).astype(jnp.bfloat16)


def block_levels(rng, extent, cuts, smallest, high):
    level = 1.0
    for position, parts in cuts:
        draws = jax.random.uniform(jax.random.fold_in(jax.random.fold_in(rng, 6), position), (parts,), jnp.float32, smallest / len(cuts), high / len(cuts))
        level = level * jnp.repeat(jnp.exp(draws), extent[position] // parts).reshape((-1,) + (1,) * (len(extent) - 1 - position))
    return level


def scatter_about(rng, extent, deviation, most, pieces=(), kind=jnp.bfloat16):
    entries = deviation * jax.random.normal(rng, extent, jnp.float32)
    if pieces:
        entries = entries * block_levels(rng, extent, pieces, -0.22, 0.18)
    return jnp.clip(entries, -most, most).astype(kind)


def setup_inputs(seed: int = 0) -> dict:
    splits = jax.random.split(jax.random.key(seed), 5)
    return {
        "inputs": scatter_about(splits[0], (MEMBERS, LAT, LON, C), 1.0, 6.0, ((0, 2), (1, 2), (2, 8))),
        "cotangent": scatter_about(splits[1], (MEMBERS, LAT, LON, C), 1.0, 6.0, ((0, 2), (1, 2), (2, 8))),
        "dw_kernel": draw_dw_kernel(jax.random.fold_in(splits[4], 71), 0),
        "pw_weight": scatter_about(splits[3], (LAYERS, C, C), C ** -0.5, 0.25),
    }


def widen(grid_field):
    periodic_field = jnp.concatenate([grid_field[:, -KERNEL_SPACING:], grid_field, grid_field[:, :KERNEL_SPACING]], axis=1)
    return jnp.pad(periodic_field, ((KERNEL_SPACING, KERNEL_SPACING), (0, 0), (0, 0)))

def stencil(padded_field, kernel, reversed_kernel):
    latitude_row_count = padded_field.shape[-3] - 2 * KERNEL_SPACING
    longitude_column_count = padded_field.shape[-2] - 2 * KERNEL_SPACING
    summed = jnp.zeros(padded_field.shape[:-3] + (latitude_row_count, longitude_column_count, padded_field.shape[-1]), jnp.float32)
    for padding_amount in range(3):
        for tap_position in range(3):
            row_shift = KERNEL_SPACING * (2 - padding_amount) if reversed_kernel else KERNEL_SPACING * padding_amount
            column_shift = KERNEL_SPACING * (2 - tap_position) if reversed_kernel else KERNEL_SPACING * tap_position
            stencil_window = padded_field[..., row_shift:row_shift + latitude_row_count, column_shift:column_shift + longitude_column_count, :].astype(jnp.float32)
            summed = summed + stencil_window * kernel[3 * padding_amount + tap_position].astype(jnp.float32)
    return summed

def normalize(conv_out):
    mean_sq = lax.optimization_barrier(jnp.mean(conv_out * conv_out, axis=-1, keepdims=True)) + 1e-06
    recip = lax.rsqrt(mean_sq)
    return (conv_out * recip, recip)

def forward_block(padded_field, kernel, weight):
    conv_out = stencil(padded_field, kernel, False)
    normed, recip = normalize(conv_out)
    hidden = normed.astype(jnp.bfloat16)
    width_c = hidden.shape[-1]
    pre_act = jnp.dot(hidden.reshape(-1, width_c), weight, preferred_element_type=jnp.float32).reshape(hidden.shape)
    interior_region = padded_field[..., KERNEL_SPACING:-KERNEL_SPACING, KERNEL_SPACING:-KERNEL_SPACING, :]
    output = (interior_region.astype(jnp.float32) + jax.nn.gelu(pre_act)).astype(jnp.bfloat16)
    return (output, hidden, pre_act, normed, recip)

def backward_block(padded_field, kernel, weight, saved, upstream, widen_fn):
    hidden, pre_act, normed, recip = saved
    _, pullback = jax.vjp(jax.nn.gelu, pre_act)
    grad_pre = pullback(upstream.astype(jnp.float32))[0].astype(jnp.bfloat16)
    width_c = hidden.shape[-1]
    flat_hidden = hidden.reshape(-1, width_c)
    flat_grad = grad_pre.reshape(-1, width_c)
    weight_term = lax.dot_general(flat_hidden, flat_grad, (((0,), (0,)), ((), ())), preferred_element_type=jnp.float32)
    grad_norm = lax.dot_general(flat_grad, weight, (((1,), (1,)), ((), ())), preferred_element_type=jnp.float32).reshape(hidden.shape)
    grad_conv = recip * (grad_norm - normed * lax.optimization_barrier(jnp.mean(grad_norm * normed, axis=-1, keepdims=True)))
    grad_conv = grad_conv.astype(jnp.bfloat16)
    latitude_row_count, longitude_column_count = (hidden.shape[-3], hidden.shape[-2])
    grad_wide = grad_conv.astype(jnp.float32)
    tap_sums = []
    for padding_amount in range(3):
        for tap_position in range(3):
            stencil_window = padded_field[..., KERNEL_SPACING * padding_amount:KERNEL_SPACING * padding_amount + latitude_row_count, KERNEL_SPACING * tap_position:KERNEL_SPACING * tap_position + longitude_column_count, :].astype(jnp.float32)
            tap_sums.append(lax.optimization_barrier(jnp.sum((stencil_window * grad_wide).reshape(-1, width_c), axis=0)))
    kernel_term = jnp.stack(tap_sums)
    back_in = upstream.astype(jnp.float32) + stencil(widen_fn(grad_conv), kernel, True)
    return (back_in.astype(jnp.bfloat16), kernel_term, weight_term)

def reference(inputs, cotangent, dw_kernel, pw_weight):

    def per_member(pair):
        member_in, member_cot = pair
        padded_in = widen(member_in)
        first = forward_block(padded_in, dw_kernel[0], pw_weight[0])
        padded_mid = widen(first[0])
        second = forward_block(padded_mid, dw_kernel[1], pw_weight[1])
        grad_mid, kernel_b, weight_b = backward_block(padded_mid, dw_kernel[1], pw_weight[1], second[1:], member_cot, widen)
        grad_in, kernel_a, weight_a = backward_block(padded_in, dw_kernel[0], pw_weight[0], first[1:], grad_mid, widen)
        return (grad_in, jnp.stack([kernel_a, kernel_b]), jnp.stack([weight_a, weight_b]))
    input_grad, kernel_terms, weight_terms = lax.map(per_member, (inputs, cotangent))
    factor = 1.0 / math.sqrt(SAMPLES)
    return (input_grad, lax.optimization_barrier(jnp.sum(kernel_terms, axis=0)) * factor, lax.optimization_barrier(jnp.sum(weight_terms, axis=0)) * factor)
```

```python
import functools
import math

import jax
import jax.numpy as jnp
from jax import lax
from jax.experimental import pallas as pl
from jax.experimental.pallas import tpu as pltpu
from jax.sharding import PartitionSpec as P

S = 4
F32 = jnp.float32
BF16 = jnp.bfloat16
MESH = pl.DeviceIdType.MESH
ROOT = math.sqrt(2.0 / math.pi)
CUBE = 0.044715


def gelu(x):
    return 0.5 * x * (1.0 + jnp.tanh(ROOT * (x + CUBE * (x * x * x))))


def gelu_slope(x):
    xx = x * x
    t = jnp.tanh(ROOT * (x + CUBE * (x * xx)))
    return 0.5 * (1.0 + t) + (0.5 * ROOT) * x * (1.0 - t * t) * (1.0 + (3.0 * CUBE) * xx)


def kernel(
    n, factor,
    x_hbm, cot_hbm, dw_ref, w_ref,
    out_hbm, kgrad, wgrad,
    raw, cotraw, u0p, u1p, g1p, g0p, g1, hid0, hid1, gp, d0, rc0, rc1, pre,
    perm, unperm, kb, kacc, wacc,
    w0s, w0r, w1s, w1r, w2s, w2r, w3s, w3r, kv, kr0, ks1, kr1, ks2, kr2,
    in_sem, out_sem, rim_s, rim_r, red_s, red_r,
):
    R, A, T, C = hid0.shape
    M = A * T
    H = C // 2
    ch = max(c for c in (1, 2, 4) if A % c == 0)
    groups = [slice(g, g + 128) for g in range(0, C, 128)]
    me, lat, mem = lax.axis_index("lon"), lax.axis_index("lat"), lax.axis_index("mem")
    other, omem = 1 - lat, 1 - mem

    def lon_at(d):
        return lax.rem(me + (d % n), n)

    def dev(lon_i, lat_i, mem_i):
        return {"lon": lon_i, "lat": lat_i, "mem": mem_i}

    def remote(src, dst, ssem, rsem, where):
        c = pltpu.make_async_remote_copy(
            src_ref=src, dst_ref=dst, send_sem=ssem, recv_sem=rsem, device_id=where, device_id_type=MESH
        )
        c.start()
        return c

    in_copies = []
    for i, (src, dst) in enumerate(((x_hbm, raw), (cot_hbm, cotraw))):
        for r in range(R):
            c = pltpu.make_async_copy(src.at[0, pl.ds(S * r, S)], dst.at[pl.ds(S * r, S)], in_sem.at[i, r])
            c.start()
            in_copies.append(c)

    barrier = pltpu.get_barrier_semaphore()
    for d in range(n):
        for la in (lat, other):
            if d == 0 and la is lat:
                continue
            pl.semaphore_signal(barrier, inc=1, device_id=dev(lon_at(d), la, mem), device_id_type=MESH)
    pl.semaphore_signal(barrier, inc=1, device_id=dev(me, lat, omem), device_id_type=MESH)

    def one_hot(rows_dim):
        o = lax.broadcasted_iota(jnp.int32, (M, M), rows_dim)
        i = lax.broadcasted_iota(jnp.int32, (M, M), 1 - rows_dim)
        a, s, b = o >> 4, (o >> 2) & 3, o & 3
        return jnp.where(i == s * (A * S) + a * S + b, 1.0, 0.0).astype(BF16)

    perm[...] = one_hot(0)
    unperm[...] = one_hot(1)
    for l in range(2):
        taps_f = dw_ref[l].astype(F32)
        for t in range(9):
            kb[l, t] = jnp.broadcast_to(taps_f[t : t + 1, :], (8, C))
    kacc[...] = jnp.zeros_like(kacc)
    kv[...] = jnp.zeros_like(kv)
    edge = lat * (R + 1)
    for ref in (u0p, u1p, g1p, g0p):
        ref[edge] = jnp.zeros(ref.shape[1:], BF16)

    def regroup(src, r):
        rows = src[pl.ds(S * r, S)].reshape(M, C)
        return jnp.dot(perm[...], rows, preferred_element_type=F32).astype(BF16).reshape(A, T, C)

    for r in range(R):
        in_copies[r].wait()
        u0p[1 + r, 1 : A + 1] = regroup(raw, r)

    pl.semaphore_wait(barrier, 2 * n)

    def rims(ref, e):
        right, left = lon_at(1), lon_at(-1)
        row = R - lat * (R - 1)
        moves = (
            (ref.at[pl.ds(1, R), pl.ds(A, 1)], ref.at[pl.ds(1, R), pl.ds(0, 1)], dev(right, lat, mem)),
            (ref.at[pl.ds(1, R), pl.ds(1, 1)], ref.at[pl.ds(1, R), pl.ds(A + 1, 1)], dev(left, lat, mem)),
            (ref.at[row, pl.ds(1, A)], ref.at[edge, pl.ds(1, A)], dev(me, other, mem)),
            (ref.at[row, pl.ds(A, 1)], ref.at[edge, pl.ds(0, 1)], dev(right, other, mem)),
            (ref.at[row, pl.ds(1, 1)], ref.at[edge, pl.ds(A + 1, 1)], dev(left, other, mem)),
        )
        return [remote(s, d, rim_s.at[e, i], rim_r.at[e, i], w) for i, (s, d, w) in enumerate(moves)]

    def finish(copies):
        for c in copies:
            c.wait()

    def wide(v):
        return v.astype(F32).reshape(2 * ch, 8, 128)

    def tap(ref, r, a, t, lanes, rev):
        p, q = divmod(t, 3)
        if rev:
            p, q = 2 - p, 2 - q
        return wide(ref[r + p, pl.ds(a + q, ch), :, lanes])

    def chunks(fn):
        def step(i, c):
            fn(i * ch)
            return c

        lax.fori_loop(0, A // ch, step, 0)

    def rows_loop(lo, hi, fn):
        def step(r, c):
            fn(r)
            return c

        lax.fori_loop(lo, hi, step, 0)

    def conv_norm(src, l, r, hid, rc, rr):
        def go(a):
            convs = []
            for lanes in groups:
                acc = tap(src, r, a, 0, lanes, False) * kb[l, 0, :, lanes]
                for t in range(1, 9):
                    acc = acc + tap(src, r, a, t, lanes, False) * kb[l, t, :, lanes]
                convs.append(acc)
            sq = sum(c * c for c in convs)
            recip = lax.rsqrt(jnp.sum(sq, axis=-1, keepdims=True) * (1.0 / C) + 1e-6)
            recip = jnp.broadcast_to(recip, (2 * ch, 8, 128))
            rc[rr, pl.ds(a, ch)] = recip.reshape(ch, T, 128)
            for lanes, c in zip(groups, convs):
                hid[r, pl.ds(a, ch), :, lanes] = (c * recip).reshape(ch, T, 128).astype(BF16)

        chunks(go)

    def mix(v, l):
        return jnp.dot(v.reshape(M, C), w_ref[l], preferred_element_type=F32).reshape(A, T, C)

    def mix_back(v, l):
        return lax.dot_general(
            v.reshape(M, C), w_ref[l], (((1,), (1,)), ((), ())), preferred_element_type=F32
        ).reshape(A, T, C)

    def norm_back(dst, hid, rc, r, rr):
        def go(a):
            ns = [wide(hid[r, pl.ds(a, ch), :, lanes]) for lanes in groups]
            gs = [pre[pl.ds(a, ch), :, lanes].reshape(2 * ch, 8, 128) for lanes in groups]
            dots = sum(g * v for g, v in zip(gs, ns))
            mean = jnp.sum(dots, axis=-1, keepdims=True) * (1.0 / C)
            recip = rc[rr, pl.ds(a, ch)].reshape(2 * ch, 8, 128)
            for lanes, g, v in zip(groups, gs, ns):
                dst[1 + r, pl.ds(1 + a, ch), :, lanes] = (recip * (g - v * mean)).reshape(ch, T, 128).astype(BF16)

        chunks(go)

    def weight_sum(l, hid):
        wacc[l] = jnp.zeros((C, C), F32)

        def go(r):
            wacc[l] += lax.dot_general(
                hid[r].reshape(M, C), gp[r].reshape(M, C), (((0,), (0,)), ((), ())), preferred_element_type=F32
            )

        rows_loop(0, R, go)

    own_rows = pl.ds(pl.multiple_of(lat * H, H), H)
    other_rows = pl.ds(pl.multiple_of(other * H, H), H)
    own_cols = pl.ds(pl.multiple_of(mem * H, H), H)
    other_cols = pl.ds(pl.multiple_of(omem * H, H), H)
    piece = H // n
    wire = w2s.dtype

    def red(l, stage, i, src, dst, where):
        return remote(src, dst, red_s.at[l, stage, i], red_r.at[l, stage, i], where)

    def stage0(l):
        w0s[l] = wacc[l, other_rows, :].astype(BF16)
        out = [red(l, 0, 0, w0s.at[l], w0r.at[l], dev(me, other, mem))]
        if l == 0:
            for k in range(2):
                for t in range(9):
                    kv[k, t : t + 1, :] = jnp.sum(kacc[k, t], axis=0, keepdims=True)
            out.append(red(l, 0, 1, kv, kr0, dev(me, other, mem)))
        return out

    def stage1(l):
        wacc[l, own_rows, :] += w0r[l].astype(F32)
        w1s[l] = wacc[l, own_rows, other_cols].astype(BF16)
        out = [red(l, 1, 0, w1s.at[l], w1r.at[l], dev(me, lat, omem))]
        if l == 0:
            kv[...] += kr0[...]
            ks1[...] = kv[:, :, other_cols]
            out.append(red(l, 1, 1, ks1, kr1, dev(me, lat, omem)))
        return out

    def stage2(l):
        total = wacc[l, own_rows, own_cols] + w1r[l].astype(F32)
        wacc[l, own_rows, own_cols] = total
        w2s[l] = total.reshape(n, piece, H).astype(wire)
        out = []
        if l == 0:
            both = kv[:, :, own_cols] + kr1[...]
            ks2[...] = both
            kr2[me] = both
        for d in range(1, n):
            to = lon_at(d)
            out.append(red(l, 2, d, w2s.at[l, to], w2r.at[l, me], dev(to, lat, mem)))
            if l == 0:
                out.append(red(l, 2, n + d, ks2, kr2.at[me], dev(to, lat, mem)))
        return out

    def stage3(l):
        start = pl.multiple_of(lat * H + me * piece, piece)
        total = wacc[l, pl.ds(start, piece), own_cols]
        for d in range(1, n):
            total = total + w2r[l, lon_at(d)].astype(F32)
        done = (total * factor).astype(wire)
        w3s[l] = done
        w3r[l, lat, me] = done
        out = []
        for d in range(n):
            for k, la in enumerate((lat, other)):
                if d or k:
                    out.append(red(l, 3, k * n + d, w3s.at[l], w3r.at[l, lat, me], dev(lon_at(d), la, mem)))
        if l == 0:
            ks = kr2[0]
            for j in range(1, n):
                ks = ks + kr2[j]
            for k in range(2):
                kgrad[k] = ks[k, :9, :] * factor
        return out

    def stage4(l):
        wgrad[l] = w3r[l].reshape(C, H).astype(F32)

    moving = rims(u0p, 0)
    for r in range(R):
        in_copies[R + r].wait()
        g1[r] = regroup(cotraw, r)
    finish(moving)

    def block0(r):
        conv_norm(u0p, 0, r, hid0, rc0, r)
        d0[r] = mix(hid0[r], 0)

        def go(a):
            for lanes in groups:
                x = d0[r, pl.ds(a, ch), :, lanes]
                u = u0p[1 + r, pl.ds(1 + a, ch), :, lanes].astype(F32)
                u1p[1 + r, pl.ds(1 + a, ch), :, lanes] = (u + gelu(x)).astype(BF16)

        chunks(go)

    rows_loop(0, R, block0)
    moving = rims(u1p, 1)

    def slopes(r):
        def go(a):
            for lanes in groups:
                d0[r, pl.ds(a, ch), :, lanes] = gelu_slope(d0[r, pl.ds(a, ch), :, lanes])

        chunks(go)

    rows_loop(0, R, slopes)
    finish(moving)

    def block1(r):
        conv_norm(u1p, 1, r, hid1, rc1, 0)
        pre[...] = mix(hid1[r], 1)

        def go(a):
            for lanes in groups:
                g = g1[r, pl.ds(a, ch), :, lanes].astype(F32)
                gp[r, pl.ds(a, ch), :, lanes] = (g * gelu_slope(pre[pl.ds(a, ch), :, lanes])).astype(BF16)

        chunks(go)
        pre[...] = mix_back(gp[r], 1)
        norm_back(g1p, hid1, rc1, r, 0)

    rows_loop(0, R, block1)
    moving = rims(g1p, 2)
    weight_sum(1, hid1)
    sums = stage0(1)
    finish(moving)

    def back0(r):
        def go(a):
            for lanes in groups:
                s = wide(g1[r, pl.ds(a, ch), :, lanes])
                u = wide(u1p[1 + r, pl.ds(1 + a, ch), :, lanes])
                for t in range(9):
                    v = tap(g1p, r, a, t, lanes, True)
                    s = s + v * kb[1, t, :, lanes]
                    kacc[1, t, :, lanes] += jnp.sum(v * u, axis=0)
                g = s.reshape(ch, T, 128).astype(BF16)
                g1[r, pl.ds(a, ch), :, lanes] = g
                gp[r, pl.ds(a, ch), :, lanes] = (g.astype(F32) * d0[r, pl.ds(a, ch), :, lanes]).astype(BF16)

        chunks(go)
        pre[...] = mix_back(gp[r], 0)
        norm_back(g0p, hid0, rc0, r, r)

    cuts = [(R * i) // 3 for i in range(4)]
    for i, stage in enumerate((stage1, stage2, stage3)):
        rows_loop(cuts[i], cuts[i + 1], back0)
        finish(sums)
        sums = stage(1)
    moving = rims(g0p, 3)
    weight_sum(0, hid0)

    def taps0(r):
        def go(a):
            for lanes in groups:
                g = wide(g0p[1 + r, pl.ds(1 + a, ch), :, lanes])
                for t in range(9):
                    kacc[0, t, :, lanes] += jnp.sum(tap(u0p, r, a, t, lanes, False) * g, axis=0)

        chunks(go)

    rows_loop(0, R, taps0)
    finish(sums)
    stage4(1)
    sums = stage0(0)
    finish(moving)

    def last(r):
        def go(a):
            for lanes in groups:
                s = wide(g1[r, pl.ds(a, ch), :, lanes])
                for t in range(9):
                    s = s + tap(g0p, r, a, t, lanes, True) * kb[0, t, :, lanes]
                hid1[r, pl.ds(a, ch), :, lanes] = s.reshape(ch, T, 128).astype(BF16)

        chunks(go)
        rows = jnp.dot(unperm[...], hid1[r].reshape(M, C), preferred_element_type=F32).astype(BF16)
        raw[pl.ds(S * r, S)] = rows.reshape(S, S * A, C)

    out_copies = []
    for i, stage in enumerate((stage1, stage2, stage3)):
        rows_loop(cuts[i], cuts[i + 1], last)
        for r in range(cuts[i], cuts[i + 1]):
            c = pltpu.make_async_copy(raw.at[pl.ds(S * r, S)], out_hbm.at[0, pl.ds(S * r, S)], out_sem.at[r])
            c.start()
            out_copies.append(c)
        finish(sums)
        sums = stage(0)
    finish(sums)
    stage4(0)
    finish(out_copies)


def body(inputs, cotangent, dw_kernel, pw_weight):
    _, rows, cols, C = inputs.shape
    n = lax.axis_size("lon")
    R, A, T, H = rows // S, cols // S, S * S, C // 2
    piece = H // n
    wire = BF16 if piece % 16 == 0 else F32
    samples = inputs.size // C * n * lax.axis_size("lat") * lax.axis_size("mem")
    anywhere = pl.BlockSpec(memory_space=pl.ANY)
    local = pl.BlockSpec(memory_space=pltpu.VMEM)
    padded = pltpu.VMEM((R + 2, A + 2, T, C), BF16)
    cells = pltpu.VMEM((R, A, T, C), BF16)
    scratch = [
        pltpu.VMEM((rows, cols, C), BF16),
        pltpu.VMEM((rows, cols, C), BF16),
        padded, padded, padded, padded,
        cells, cells, cells, cells,
        pltpu.VMEM((R, A, T, C), F32),
        pltpu.VMEM((R, A, T, 128), F32),
        pltpu.VMEM((1, A, T, 128), F32),
        pltpu.VMEM((A, T, C), F32),
        pltpu.VMEM((A * T, A * T), BF16),
        pltpu.VMEM((A * T, A * T), BF16),
        pltpu.VMEM((2, 9, 8, C), F32),
        pltpu.VMEM((2, 9, 8, C), F32),
        pltpu.VMEM((2, C, C), F32),
        pltpu.VMEM((2, H, C), BF16), pltpu.VMEM((2, H, C), BF16),
        pltpu.VMEM((2, H, H), BF16), pltpu.VMEM((2, H, H), BF16),
        pltpu.VMEM((2, n, piece, H), wire), pltpu.VMEM((2, n, piece, H), wire),
        pltpu.VMEM((2, piece, H), wire), pltpu.VMEM((2, 2, n, piece, H), wire),
        pltpu.VMEM((2, 16, C), F32), pltpu.VMEM((2, 16, C), F32),
        pltpu.VMEM((2, 16, H), F32), pltpu.VMEM((2, 16, H), F32),
        pltpu.VMEM((2, 16, H), F32), pltpu.VMEM((n, 2, 16, H), F32),
        pltpu.SemaphoreType.DMA((2, R)), pltpu.SemaphoreType.DMA((R,)),
        pltpu.SemaphoreType.DMA((4, 5)), pltpu.SemaphoreType.DMA((4, 5)),
        pltpu.SemaphoreType.DMA((2, 4, 2 * n)), pltpu.SemaphoreType.DMA((2, 4, 2 * n)),
    ]
    return pl.pallas_call(
        functools.partial(kernel, n, 1.0 / math.sqrt(samples)),
        out_shape=(
            jax.ShapeDtypeStruct(inputs.shape, BF16),
            jax.ShapeDtypeStruct((2, 9, H), F32),
            jax.ShapeDtypeStruct((2, C, H), F32),
        ),
        in_specs=[anywhere, anywhere, local, local],
        out_specs=(anywhere, local, local),
        scratch_shapes=scratch,
        name="blocks",
        compiler_params=pltpu.CompilerParams(
            collective_id=0, has_side_effects=True, vmem_limit_bytes=60 * 1024 * 1024
        ),
    )(inputs, cotangent, dw_kernel, pw_weight)


def solution(mesh):
    placed = (P("mem", "lat", "lon", None), P("mem", "lat", "lon", None), P(), P())
    return jax.shard_map(
        body,
        mesh=mesh,
        in_specs=placed,
        out_specs=(P("mem", "lat", "lon", None), P(None, None, "mem"), P(None, None, "mem")),
        check_vma=False,
    )
```

```python
import functools
import math

import jax
import jax.numpy as jnp
from jax import lax
from jax.experimental import pallas as pl
from jax.experimental.pallas import tpu as pltpu
from jax.sharding import PartitionSpec as P

S = 4
F32 = jnp.float32
BF16 = jnp.bfloat16
MESH = pl.DeviceIdType.MESH
ROOT = math.sqrt(2.0 / math.pi)
CUBE = 0.044715


def gelu(x):
    return 0.5 * x * (1.0 + jnp.tanh(ROOT * (x + CUBE * (x * x * x))))


def gelu_slope(x):
    xx = x * x
    t = jnp.tanh(ROOT * (x + CUBE * (x * xx)))
    return 0.5 * (1.0 + t) + (0.5 * ROOT) * x * (1.0 - t * t) * (1.0 + (3.0 * CUBE) * xx)


def kernel(
    n, factor,
    x_hbm, cot_hbm, dw_ref, w_ref,
    out_hbm, kgrad, wgrad,
    raw, cotraw, u0p, u1p, g1p, g0p, g1, hid0, hid1, gp, d0, rc0, rc1, pre,
    perm, unperm, kb, kacc, wacc,
    w0s, w0r, w1s, w1r, w2s, w2r, w3s, w3r, kv, kr0, ks1, kr1, ks2, kr2,
    in_sem, out_sem, rim_s, rim_r, red_s, red_r,
):
    R, A, T, C = hid0.shape
    M = A * T
    H = C // 2
    ch = max(c for c in (1, 2, 4) if A % c == 0)
    groups = [slice(g, g + 128) for g in range(0, C, 128)]
    me, lat, mem = lax.axis_index("lon"), lax.axis_index("lat"), lax.axis_index("mem")
    other, omem = 1 - lat, 1 - mem

    def lon_at(d):
        return lax.rem(me + (d % n), n)

    def dev(lon_i, lat_i, mem_i):
        return {"lon": lon_i, "lat": lat_i, "mem": mem_i}

    def remote(src, dst, ssem, rsem, where):
        c = pltpu.make_async_remote_copy(
            src_ref=src, dst_ref=dst, send_sem=ssem, recv_sem=rsem, device_id=where, device_id_type=MESH
        )
        c.start()
        return c

    in_copies = []
    for i, (src, dst) in enumerate(((x_hbm, raw), (cot_hbm, cotraw))):
        for r in range(R):
            c = pltpu.make_async_copy(src.at[0, pl.ds(S * r, S)], dst.at[pl.ds(S * r, S)], in_sem.at[i, r])
            c.start()
            in_copies.append(c)

    barrier = pltpu.get_barrier_semaphore()
    for d in range(n):
        for la in (lat, other):
            if d == 0 and la is lat:
                continue
            pl.semaphore_signal(barrier, inc=1, device_id=dev(lon_at(d), la, mem), device_id_type=MESH)
    pl.semaphore_signal(barrier, inc=1, device_id=dev(me, lat, omem), device_id_type=MESH)

    def one_hot(rows_dim):
        o = lax.broadcasted_iota(jnp.int32, (M, M), rows_dim)
        i = lax.broadcasted_iota(jnp.int32, (M, M), 1 - rows_dim)
        a, s, b = o >> 4, (o >> 2) & 3, o & 3
        return jnp.where(i == s * (A * S) + a * S + b, 1.0, 0.0).astype(BF16)

    perm[...] = one_hot(0)
    unperm[...] = one_hot(1)
    for l in range(2):
        taps_f = dw_ref[l].astype(F32)
        for t in range(9):
            kb[l, t] = jnp.broadcast_to(taps_f[t : t + 1, :], (8, C))
    kacc[...] = jnp.zeros_like(kacc)
    kv[...] = jnp.zeros_like(kv)
    edge = lat * (R + 1)
    for ref in (u0p, u1p, g1p, g0p):
        ref[edge] = jnp.zeros(ref.shape[1:], BF16)

    def regroup(src, r):
        rows = src[pl.ds(S * r, S)].reshape(M, C)
        return jnp.dot(perm[...], rows, preferred_element_type=F32).astype(BF16).reshape(A, T, C)

    for r in range(R):
        in_copies[r].wait()
        u0p[1 + r, 1 : A + 1] = regroup(raw, r)

    pl.semaphore_wait(barrier, 2 * n)

    def rims(ref, e):
        right, left = lon_at(1), lon_at(-1)
        row = R - lat * (R - 1)
        moves = (
            (ref.at[pl.ds(1, R), pl.ds(A, 1)], ref.at[pl.ds(1, R), pl.ds(0, 1)], dev(right, lat, mem)),
            (ref.at[pl.ds(1, R), pl.ds(1, 1)], ref.at[pl.ds(1, R), pl.ds(A + 1, 1)], dev(left, lat, mem)),
            (ref.at[row, pl.ds(1, A)], ref.at[edge, pl.ds(1, A)], dev(me, other, mem)),
            (ref.at[row, pl.ds(A, 1)], ref.at[edge, pl.ds(0, 1)], dev(right, other, mem)),
            (ref.at[row, pl.ds(1, 1)], ref.at[edge, pl.ds(A + 1, 1)], dev(left, other, mem)),
        )
        return [remote(s, d, rim_s.at[e, i], rim_r.at[e, i], w) for i, (s, d, w) in enumerate(moves)]

    def finish(copies):
        for c in copies:
            c.wait()

    def wide(v):
        return v.astype(F32).reshape(2 * ch, 8, 128)

    def taps(ref, r, a, lanes, rev):
        for p in range(3):
            row = ref[r + p, pl.ds(a, ch + 2), :, lanes].astype(F32).reshape(2 * ch + 4, 8, 128)
            for q in range(3):
                t = 3 * (2 - p) + 2 - q if rev else 3 * p + q
                yield t, row[2 * q : 2 * q + 2 * ch]

    def chunks(fn):
        def step(i, c):
            fn(i * ch)
            return c

        lax.fori_loop(0, A // ch, step, 0)

    def rows_loop(lo, hi, fn):
        def step(r, c):
            fn(r)
            return c

        lax.fori_loop(lo, hi, step, 0)

    def conv_norm(src, l, r, hid, rc, rr):
        def go(a):
            convs = []
            for lanes in groups:
                acc = 0.0
                for t, v in taps(src, r, a, lanes, False):
                    acc = acc + v * kb[l, t, :, lanes]
                convs.append(acc)
            sq = sum(c * c for c in convs)
            recip = lax.rsqrt(jnp.sum(sq, axis=-1, keepdims=True) * (1.0 / C) + 1e-6)
            recip = jnp.broadcast_to(recip, (2 * ch, 8, 128))
            rc[rr, pl.ds(a, ch)] = recip.reshape(ch, T, 128)
            for lanes, c in zip(groups, convs):
                hid[r, pl.ds(a, ch), :, lanes] = (c * recip).reshape(ch, T, 128).astype(BF16)

        chunks(go)

    def mix(v, l):
        return jnp.dot(v.reshape(M, C), w_ref[l], preferred_element_type=F32).reshape(A, T, C)

    def mix_back(v, l):
        return lax.dot_general(
            v.reshape(M, C), w_ref[l], (((1,), (1,)), ((), ())), preferred_element_type=F32
        ).reshape(A, T, C)

    def norm_back(dst, hid, rc, r, rr):
        def go(a):
            ns = [wide(hid[r, pl.ds(a, ch), :, lanes]) for lanes in groups]
            gs = [pre[pl.ds(a, ch), :, lanes].reshape(2 * ch, 8, 128) for lanes in groups]
            dots = sum(g * v for g, v in zip(gs, ns))
            mean = jnp.sum(dots, axis=-1, keepdims=True) * (1.0 / C)
            recip = rc[rr, pl.ds(a, ch)].reshape(2 * ch, 8, 128)
            for lanes, g, v in zip(groups, gs, ns):
                dst[1 + r, pl.ds(1 + a, ch), :, lanes] = (recip * (g - v * mean)).reshape(ch, T, 128).astype(BF16)

        chunks(go)

    def weight_sum(l, hid):
        wacc[l] = jnp.zeros((C, C), F32)

        def go(r):
            wacc[l] += lax.dot_general(
                hid[r].reshape(M, C), gp[r].reshape(M, C), (((0,), (0,)), ((), ())), preferred_element_type=F32
            )

        rows_loop(0, R, go)

    own_rows = pl.ds(pl.multiple_of(lat * H, H), H)
    other_rows = pl.ds(pl.multiple_of(other * H, H), H)
    own_cols = pl.ds(pl.multiple_of(mem * H, H), H)
    other_cols = pl.ds(pl.multiple_of(omem * H, H), H)
    piece = H // n
    wire = w2s.dtype

    def red(l, stage, i, src, dst, where):
        return remote(src, dst, red_s.at[l, stage, i], red_r.at[l, stage, i], where)

    def stage0(l):
        w0s[l] = wacc[l, other_rows, :].astype(BF16)
        return [red(l, 0, 0, w0s.at[l], w0r.at[l], dev(me, other, mem))]

    def taps_stage0():
        for k in range(2):
            for t in range(9):
                kv[k, t : t + 1, :] = jnp.sum(kacc[k, t], axis=0, keepdims=True)
        return [red(0, 0, 1, kv, kr0, dev(me, other, mem))]

    def taps_stage1():
        kv[...] += kr0[...]
        ks1[...] = kv[:, :, other_cols]
        return [red(0, 1, 1, ks1, kr1, dev(me, lat, omem))]

    def taps_stage2():
        both = (kv[:, :, own_cols] + kr1[...]).astype(BF16)
        ks2[...] = both
        kr2[me] = both
        return [red(0, 2, n + d, ks2, kr2.at[me], dev(lon_at(d), lat, mem)) for d in range(1, n)]

    def taps_stage3():
        ks = kr2[0].astype(F32)
        for j in range(1, n):
            ks = ks + kr2[j].astype(F32)
        for k in range(2):
            kgrad[k] = ks[k, :9, :] * factor
        return []

    def stage1(l):
        wacc[l, own_rows, :] += w0r[l].astype(F32)
        w1s[l] = wacc[l, own_rows, other_cols].astype(BF16)
        return [red(l, 1, 0, w1s.at[l], w1r.at[l], dev(me, lat, omem))]

    def stage2(l):
        total = wacc[l, own_rows, own_cols] + w1r[l].astype(F32)
        wacc[l, own_rows, own_cols] = total
        w2s[l] = total.reshape(n, piece, H).astype(wire)
        return [
            red(l, 2, d, w2s.at[l, lon_at(d)], w2r.at[l, me], dev(lon_at(d), lat, mem)) for d in range(1, n)
        ]

    def stage3(l):
        start = pl.multiple_of(lat * H + me * piece, piece)
        total = wacc[l, pl.ds(start, piece), own_cols]
        for d in range(1, n):
            total = total + w2r[l, lon_at(d)].astype(F32)
        done = (total * factor).astype(wire)
        w3s[l] = done
        w3r[l, lat, me] = done
        out = []
        for d in range(n):
            for k, la in enumerate((lat, other)):
                if d or k:
                    out.append(red(l, 3, k * n + d, w3s.at[l], w3r.at[l, lat, me], dev(lon_at(d), la, mem)))
        return out

    def stage4(l):
        wgrad[l] = w3r[l].reshape(C, H).astype(F32)

    moving = rims(u0p, 0)
    for r in range(R):
        in_copies[R + r].wait()
        g1[r] = regroup(cotraw, r)
    finish(moving)

    def block0(r):
        conv_norm(u0p, 0, r, hid0, rc0, r)
        d0[r] = mix(hid0[r], 0)

        def go(a):
            for lanes in groups:
                x = d0[r, pl.ds(a, ch), :, lanes]
                u = u0p[1 + r, pl.ds(1 + a, ch), :, lanes].astype(F32)
                u1p[1 + r, pl.ds(1 + a, ch), :, lanes] = (u + gelu(x)).astype(BF16)

        chunks(go)

    rows_loop(0, R, block0)
    moving = rims(u1p, 1)

    def slopes(r):
        def go(a):
            for lanes in groups:
                d0[r, pl.ds(a, ch), :, lanes] = gelu_slope(d0[r, pl.ds(a, ch), :, lanes])

        chunks(go)

    rows_loop(0, R, slopes)
    finish(moving)

    def block1(r):
        conv_norm(u1p, 1, r, hid1, rc1, 0)
        pre[...] = mix(hid1[r], 1)

        def go(a):
            for lanes in groups:
                g = g1[r, pl.ds(a, ch), :, lanes].astype(F32)
                gp[r, pl.ds(a, ch), :, lanes] = (g * gelu_slope(pre[pl.ds(a, ch), :, lanes])).astype(BF16)

        chunks(go)
        pre[...] = mix_back(gp[r], 1)
        norm_back(g1p, hid1, rc1, r, 0)

    rows_loop(0, R, block1)
    moving = rims(g1p, 2)
    weight_sum(1, hid1)
    sums = stage0(1)
    finish(moving)

    def back0(r):
        def go(a):
            for lanes in groups:
                s = wide(g1[r, pl.ds(a, ch), :, lanes])
                u = wide(u1p[1 + r, pl.ds(1 + a, ch), :, lanes])
                for t, v in taps(g1p, r, a, lanes, True):
                    s = s + v * kb[1, t, :, lanes]
                    kacc[1, t, :, lanes] += jnp.sum(v * u, axis=0)
                g = s.reshape(ch, T, 128).astype(BF16)
                g1[r, pl.ds(a, ch), :, lanes] = g
                gp[r, pl.ds(a, ch), :, lanes] = (g.astype(F32) * d0[r, pl.ds(a, ch), :, lanes]).astype(BF16)

        chunks(go)
        pre[...] = mix_back(gp[r], 0)
        norm_back(g0p, hid0, rc0, r, r)

    cuts = [(R * i) // 3 for i in range(4)]
    for i, stage in enumerate((stage1, stage2, stage3)):
        rows_loop(cuts[i], cuts[i + 1], back0)
        finish(sums)
        sums = stage(1)
    moving = rims(g0p, 3)
    weight_sum(0, hid0)
    finish(sums)
    sums = stage0(0)

    def taps0(r):
        def go(a):
            for lanes in groups:
                g = wide(g0p[1 + r, pl.ds(1 + a, ch), :, lanes])
                for t, v in taps(u0p, r, a, lanes, False):
                    kacc[0, t, :, lanes] += jnp.sum(v * g, axis=0)

        chunks(go)

    rows_loop(0, R, taps0)
    tap_sums = taps_stage0()
    finish(sums)
    sums = stage1(0)
    stage4(1)
    finish(moving)

    def last(r):
        def go(a):
            for lanes in groups:
                s = wide(g1[r, pl.ds(a, ch), :, lanes])
                for t, v in taps(g0p, r, a, lanes, True):
                    s = s + v * kb[0, t, :, lanes]
                hid1[r, pl.ds(a, ch), :, lanes] = s.reshape(ch, T, 128).astype(BF16)

        chunks(go)
        rows = jnp.dot(unperm[...], hid1[r].reshape(M, C), preferred_element_type=F32).astype(BF16)
        raw[pl.ds(S * r, S)] = rows.reshape(S, S * A, C)

    out_copies = []
    tap_stages = (taps_stage1, taps_stage2, taps_stage3)
    for i, stage in enumerate((stage2, stage3, None)):
        rows_loop(cuts[i], cuts[i + 1], last)
        for r in range(cuts[i], cuts[i + 1]):
            c = pltpu.make_async_copy(raw.at[pl.ds(S * r, S)], out_hbm.at[0, pl.ds(S * r, S)], out_sem.at[r])
            c.start()
            out_copies.append(c)
        finish(sums)
        sums = stage(0) if stage else []
        finish(tap_sums)
        tap_sums = tap_stages[i]()
    stage4(0)
    finish(out_copies)


def body(inputs, cotangent, dw_kernel, pw_weight):
    _, rows, cols, C = inputs.shape
    n = lax.axis_size("lon")
    R, A, T, H = rows // S, cols // S, S * S, C // 2
    piece = H // n
    wire = BF16 if piece % 16 == 0 else F32
    samples = inputs.size // C * n * lax.axis_size("lat") * lax.axis_size("mem")
    anywhere = pl.BlockSpec(memory_space=pl.ANY)
    local = pl.BlockSpec(memory_space=pltpu.VMEM)
    padded = pltpu.VMEM((R + 2, A + 2, T, C), BF16)
    cells = pltpu.VMEM((R, A, T, C), BF16)
    scratch = [
        pltpu.VMEM((rows, cols, C), BF16),
        pltpu.VMEM((rows, cols, C), BF16),
        padded, padded, padded, padded,
        cells, cells, cells, cells,
        pltpu.VMEM((R, A, T, C), F32),
        pltpu.VMEM((R, A, T, 128), F32),
        pltpu.VMEM((1, A, T, 128), F32),
        pltpu.VMEM((A, T, C), F32),
        pltpu.VMEM((A * T, A * T), BF16),
        pltpu.VMEM((A * T, A * T), BF16),
        pltpu.VMEM((2, 9, 8, C), F32),
        pltpu.VMEM((2, 9, 8, C), F32),
        pltpu.VMEM((2, C, C), F32),
        pltpu.VMEM((2, H, C), BF16), pltpu.VMEM((2, H, C), BF16),
        pltpu.VMEM((2, H, H), BF16), pltpu.VMEM((2, H, H), BF16),
        pltpu.VMEM((2, n, piece, H), wire), pltpu.VMEM((2, n, piece, H), wire),
        pltpu.VMEM((2, piece, H), wire), pltpu.VMEM((2, 2, n, piece, H), wire),
        pltpu.VMEM((2, 16, C), F32), pltpu.VMEM((2, 16, C), F32),
        pltpu.VMEM((2, 16, H), F32), pltpu.VMEM((2, 16, H), F32),
        pltpu.VMEM((2, 16, H), BF16), pltpu.VMEM((n, 2, 16, H), BF16),
        pltpu.SemaphoreType.DMA((2, R)), pltpu.SemaphoreType.DMA((R,)),
        pltpu.SemaphoreType.DMA((4, 5)), pltpu.SemaphoreType.DMA((4, 5)),
        pltpu.SemaphoreType.DMA((2, 4, 2 * n)), pltpu.SemaphoreType.DMA((2, 4, 2 * n)),
    ]
    return pl.pallas_call(
        functools.partial(kernel, n, 1.0 / math.sqrt(samples)),
        out_shape=(
            jax.ShapeDtypeStruct(inputs.shape, BF16),
            jax.ShapeDtypeStruct((2, 9, H), F32),
            jax.ShapeDtypeStruct((2, C, H), F32),
        ),
        in_specs=[anywhere, anywhere, local, local],
        out_specs=(anywhere, local, local),
        scratch_shapes=scratch,
        name="blocks",
        compiler_params=pltpu.CompilerParams(
            collective_id=0, has_side_effects=True, vmem_limit_bytes=60 * 1024 * 1024
        ),
    )(inputs, cotangent, dw_kernel, pw_weight)


def solution(mesh):
    placed = (P("mem", "lat", "lon", None), P("mem", "lat", "lon", None), P(), P())
    return jax.shard_map(
        body,
        mesh=mesh,
        in_specs=placed,
        out_specs=(P("mem", "lat", "lon", None), P(None, None, "mem"), P(None, None, "mem")),
        check_vma=False,
    )
```

```python
import functools
import math

import jax
import jax.numpy as jnp
from jax import lax
from jax.experimental import pallas as pl
from jax.experimental.pallas import tpu as pltpu
from jax.sharding import PartitionSpec as P

S = 4
F32 = jnp.float32
BF16 = jnp.bfloat16
MESH = pl.DeviceIdType.MESH
ROOT = math.sqrt(2.0 / math.pi)
CUBE = 0.044715


def gelu(x):
    return 0.5 * x * (1.0 + jnp.tanh(ROOT * (x + CUBE * (x * x * x))))


def gelu_slope(x):
    xx = x * x
    t = jnp.tanh(ROOT * (x + CUBE * (x * xx)))
    return 0.5 * (1.0 + t) + (0.5 * ROOT) * x * (1.0 - t * t) * (1.0 + (3.0 * CUBE) * xx)


def kernel(
    n, factor,
    x_hbm, cot_hbm, dw_ref, w_ref,
    out_hbm, kgrad, wgrad,
    raw, cotraw, u0p, u1p, g1p, g0p, g1, hid0, hid1, gp, d0, rc0, rc1, pre,
    perm, unperm, kb, kacc, wacc,
    w0s, w0r, w1s, w1r, w2s, w2r, w3s, w3r, kv, kr0, ks1, kr1, ks2, kr2,
    in_sem, out_sem, rim_s, rim_r, red_s, red_r,
):
    R, A, T, C = hid0.shape
    M = A * T
    H = C // 2
    ch = max(c for c in (1, 2, 4) if A % c == 0)
    groups = [slice(g, g + 128) for g in range(0, C, 128)]
    me, lat, mem = lax.axis_index("lon"), lax.axis_index("lat"), lax.axis_index("mem")
    other, omem = 1 - lat, 1 - mem

    def lon_at(d):
        return lax.rem(me + (d % n), n)

    def dev(lon_i, lat_i, mem_i):
        return {"lon": lon_i, "lat": lat_i, "mem": mem_i}

    def remote(src, dst, ssem, rsem, where):
        c = pltpu.make_async_remote_copy(
            src_ref=src, dst_ref=dst, send_sem=ssem, recv_sem=rsem, device_id=where, device_id_type=MESH
        )
        c.start()
        return c

    in_copies = []
    for i, (src, dst) in enumerate(((x_hbm, raw), (cot_hbm, cotraw))):
        for r in range(R):
            c = pltpu.make_async_copy(src.at[0, pl.ds(S * r, S)], dst.at[pl.ds(S * r, S)], in_sem.at[i, r])
            c.start()
            in_copies.append(c)

    barrier = pltpu.get_barrier_semaphore()
    for d in range(n):
        for la in (lat, other):
            if d == 0 and la is lat:
                continue
            pl.semaphore_signal(barrier, inc=1, device_id=dev(lon_at(d), la, mem), device_id_type=MESH)
    pl.semaphore_signal(barrier, inc=1, device_id=dev(me, lat, omem), device_id_type=MESH)

    def one_hot(rows_dim):
        o = lax.broadcasted_iota(jnp.int32, (M, M), rows_dim)
        i = lax.broadcasted_iota(jnp.int32, (M, M), 1 - rows_dim)
        a, s, b = o >> 4, (o >> 2) & 3, o & 3
        return jnp.where(i == s * (A * S) + a * S + b, 1.0, 0.0).astype(BF16)

    perm[...] = one_hot(0)
    unperm[...] = one_hot(1)
    for l in range(2):
        taps_f = dw_ref[l].astype(F32)
        for t in range(9):
            kb[l, t] = jnp.broadcast_to(taps_f[t : t + 1, :], (8, C))
    kacc[...] = jnp.zeros_like(kacc)
    kv[...] = jnp.zeros_like(kv)
    edge = lat * (R + 1)
    for ref in (u0p, u1p, g1p, g0p):
        ref[edge] = jnp.zeros(ref.shape[1:], BF16)

    def regroup(src, r):
        rows = src[pl.ds(S * r, S)].reshape(M, C)
        return jnp.dot(perm[...], rows, preferred_element_type=F32).astype(BF16).reshape(A, T, C)

    for r in range(R):
        in_copies[r].wait()
        u0p[1 + r, 1 : A + 1] = regroup(raw, r)

    pl.semaphore_wait(barrier, 2 * n)

    right, left = lon_at(1), lon_at(-1)

    def send_rims(e, first, moves):
        return [
            remote(s, d, rim_s.at[e, i + first], rim_r.at[e, i + first], w) for i, (s, d, w) in enumerate(moves)
        ]

    def lon_rims(ref, e):
        moves = (
            (ref.at[pl.ds(1, R), pl.ds(A, 1)], ref.at[pl.ds(1, R), pl.ds(0, 1)], dev(right, lat, mem)),
            (ref.at[pl.ds(1, R), pl.ds(1, 1)], ref.at[pl.ds(1, R), pl.ds(A + 1, 1)], dev(left, lat, mem)),
        )
        return send_rims(e, 0, moves)

    def lat_rims(ref, e):
        row = R - lat * (R - 1)
        moves = (
            (ref.at[row, pl.ds(1, A)], ref.at[edge, pl.ds(1, A)], dev(me, other, mem)),
            (ref.at[row, pl.ds(A, 1)], ref.at[edge, pl.ds(0, 1)], dev(right, other, mem)),
            (ref.at[row, pl.ds(1, 1)], ref.at[edge, pl.ds(A + 1, 1)], dev(left, other, mem)),
        )
        return send_rims(e, 2, moves)

    def inward(i):
        return i + other * (R - 1 - 2 * i)

    def finish(copies):
        for c in copies:
            c.wait()

    def wide(v):
        return v.astype(F32).reshape(2 * ch, 8, 128)

    def taps(ref, r, a, lanes, rev):
        for p in range(3):
            row = ref[r + p, pl.ds(a, ch + 2), :, lanes].astype(F32).reshape(2 * ch + 4, 8, 128)
            for q in range(3):
                t = 3 * (2 - p) + 2 - q if rev else 3 * p + q
                yield t, row[2 * q : 2 * q + 2 * ch]

    def chunks(fn):
        def step(i, c):
            fn(i * ch)
            return c

        lax.fori_loop(0, A // ch, step, 0)

    def rows_loop(lo, hi, fn):
        def step(r, c):
            fn(r)
            return c

        lax.fori_loop(lo, hi, step, 0)

    def conv_norm(src, l, r, hid, rc, rr):
        def go(a):
            convs = []
            for lanes in groups:
                acc = 0.0
                for t, v in taps(src, r, a, lanes, False):
                    acc = acc + v * kb[l, t, :, lanes]
                convs.append(acc)
            sq = sum(c * c for c in convs)
            recip = lax.rsqrt(jnp.sum(sq, axis=-1, keepdims=True) * (1.0 / C) + 1e-6)
            recip = jnp.broadcast_to(recip, (2 * ch, 8, 128))
            rc[rr, pl.ds(a, ch)] = recip.reshape(ch, T, 128)
            for lanes, c in zip(groups, convs):
                hid[r, pl.ds(a, ch), :, lanes] = (c * recip).reshape(ch, T, 128).astype(BF16)

        chunks(go)

    def mix(v, l):
        return jnp.dot(v.reshape(M, C), w_ref[l], preferred_element_type=F32).reshape(A, T, C)

    def mix_back(v, l):
        return lax.dot_general(
            v.reshape(M, C), w_ref[l], (((1,), (1,)), ((), ())), preferred_element_type=F32
        ).reshape(A, T, C)

    def norm_back(dst, hid, rc, r, rr):
        def go(a):
            ns = [wide(hid[r, pl.ds(a, ch), :, lanes]) for lanes in groups]
            gs = [pre[pl.ds(a, ch), :, lanes].reshape(2 * ch, 8, 128) for lanes in groups]
            dots = sum(g * v for g, v in zip(gs, ns))
            mean = jnp.sum(dots, axis=-1, keepdims=True) * (1.0 / C)
            recip = rc[rr, pl.ds(a, ch)].reshape(2 * ch, 8, 128)
            for lanes, g, v in zip(groups, gs, ns):
                dst[1 + r, pl.ds(1 + a, ch), :, lanes] = (recip * (g - v * mean)).reshape(ch, T, 128).astype(BF16)

        chunks(go)

    def weight_sum(l, hid):
        wacc[l] = jnp.zeros((C, C), F32)

        def go(r):
            wacc[l] += lax.dot_general(
                hid[r].reshape(M, C), gp[r].reshape(M, C), (((0,), (0,)), ((), ())), preferred_element_type=F32
            )

        rows_loop(0, R, go)

    own_rows = pl.ds(pl.multiple_of(lat * H, H), H)
    other_rows = pl.ds(pl.multiple_of(other * H, H), H)
    own_cols = pl.ds(pl.multiple_of(mem * H, H), H)
    other_cols = pl.ds(pl.multiple_of(omem * H, H), H)
    piece = H // n
    wire = w2s.dtype

    def red(l, stage, i, src, dst, where):
        return remote(src, dst, red_s.at[l, stage, i], red_r.at[l, stage, i], where)

    def stage0(l):
        w0s[l] = wacc[l, other_rows, :].astype(BF16)
        return [red(l, 0, 0, w0s.at[l], w0r.at[l], dev(me, other, mem))]

    def taps_stage0():
        for k in range(2):
            for t in range(9):
                kv[k, t : t + 1, :] = jnp.sum(kacc[k, t], axis=0, keepdims=True)
        return [red(0, 0, 1, kv, kr0, dev(me, other, mem))]

    def taps_stage1():
        kv[...] += kr0[...]
        ks1[...] = kv[:, :, other_cols]
        return [red(0, 1, 1, ks1, kr1, dev(me, lat, omem))]

    def taps_stage2():
        both = (kv[:, :, own_cols] + kr1[...]).astype(BF16)
        ks2[...] = both
        kr2[me] = both
        return [red(0, 2, n + d, ks2, kr2.at[me], dev(lon_at(d), lat, mem)) for d in range(1, n)]

    def taps_stage3():
        ks = kr2[0].astype(F32)
        for j in range(1, n):
            ks = ks + kr2[j].astype(F32)
        for k in range(2):
            kgrad[k] = ks[k, :9, :] * factor
        return []

    def stage1(l):
        wacc[l, own_rows, :] += w0r[l].astype(F32)
        w1s[l] = wacc[l, own_rows, other_cols].astype(BF16)
        return [red(l, 1, 0, w1s.at[l], w1r.at[l], dev(me, lat, omem))]

    def stage2(l):
        total = wacc[l, own_rows, own_cols] + w1r[l].astype(F32)
        wacc[l, own_rows, own_cols] = total
        w2s[l] = total.reshape(n, piece, H).astype(wire)
        return [
            red(l, 2, d, w2s.at[l, lon_at(d)], w2r.at[l, me], dev(lon_at(d), lat, mem)) for d in range(1, n)
        ]

    def stage3(l):
        start = pl.multiple_of(lat * H + me * piece, piece)
        total = wacc[l, pl.ds(start, piece), own_cols]
        for d in range(1, n):
            total = total + w2r[l, lon_at(d)].astype(F32)
        done = (total * factor).astype(wire)
        w3s[l] = done
        w3r[l, lat, me] = done
        out = []
        for d in range(n):
            for k, la in enumerate((lat, other)):
                if d or k:
                    out.append(red(l, 3, k * n + d, w3s.at[l], w3r.at[l, lat, me], dev(lon_at(d), la, mem)))
        return out

    def stage4(l):
        wgrad[l] = w3r[l].reshape(C, H).astype(F32)

    moving = lat_rims(u0p, 0) + lon_rims(u0p, 0)
    for r in range(R):
        in_copies[R + r].wait()
        g1[r] = regroup(cotraw, r)
    finish(moving)

    def block0(i):
        r = inward(i)
        conv_norm(u0p, 0, r, hid0, rc0, r)
        d0[r] = mix(hid0[r], 0)

        def go(a):
            for lanes in groups:
                x = d0[r, pl.ds(a, ch), :, lanes]
                u = u0p[1 + r, pl.ds(1 + a, ch), :, lanes].astype(F32)
                u1p[1 + r, pl.ds(1 + a, ch), :, lanes] = (u + gelu(x)).astype(BF16)

        chunks(go)

    rows_loop(0, 1, block0)
    moving = lat_rims(u1p, 1)
    rows_loop(1, R, block0)
    moving += lon_rims(u1p, 1)

    def slopes(r):
        def go(a):
            for lanes in groups:
                d0[r, pl.ds(a, ch), :, lanes] = gelu_slope(d0[r, pl.ds(a, ch), :, lanes])

        chunks(go)

    rows_loop(0, R, slopes)
    finish(moving)

    def block1(i):
        r = inward(i)
        conv_norm(u1p, 1, r, hid1, rc1, 0)
        pre[...] = mix(hid1[r], 1)

        def go(a):
            for lanes in groups:
                g = g1[r, pl.ds(a, ch), :, lanes].astype(F32)
                gp[r, pl.ds(a, ch), :, lanes] = (g * gelu_slope(pre[pl.ds(a, ch), :, lanes])).astype(BF16)

        chunks(go)
        pre[...] = mix_back(gp[r], 1)
        norm_back(g1p, hid1, rc1, r, 0)

    rows_loop(0, 1, block1)
    moving = lat_rims(g1p, 2)
    rows_loop(1, R, block1)
    moving += lon_rims(g1p, 2)
    weight_sum(1, hid1)
    sums = stage0(1)
    finish(moving)

    def back0(i):
        r = inward(i)
        def go(a):
            for lanes in groups:
                s = wide(g1[r, pl.ds(a, ch), :, lanes])
                u = wide(u1p[1 + r, pl.ds(1 + a, ch), :, lanes])
                for t, v in taps(g1p, r, a, lanes, True):
                    s = s + v * kb[1, t, :, lanes]
                    kacc[1, t, :, lanes] += jnp.sum(v * u, axis=0)
                g = s.reshape(ch, T, 128).astype(BF16)
                g1[r, pl.ds(a, ch), :, lanes] = g
                gp[r, pl.ds(a, ch), :, lanes] = (g.astype(F32) * d0[r, pl.ds(a, ch), :, lanes]).astype(BF16)

        chunks(go)
        pre[...] = mix_back(gp[r], 0)
        norm_back(g0p, hid0, rc0, r, r)

    cuts = [(R * i) // 3 for i in range(4)]
    rows_loop(0, 1, back0)
    moving = lat_rims(g0p, 3)
    for i, stage in enumerate((stage1, stage2, stage3)):
        rows_loop(max(cuts[i], 1), cuts[i + 1], back0)
        finish(sums)
        sums = stage(1)
    moving += lon_rims(g0p, 3)
    weight_sum(0, hid0)
    finish(sums)
    sums = stage0(0)

    def taps0(r):
        def go(a):
            for lanes in groups:
                g = wide(g0p[1 + r, pl.ds(1 + a, ch), :, lanes])
                for t, v in taps(u0p, r, a, lanes, False):
                    kacc[0, t, :, lanes] += jnp.sum(v * g, axis=0)

        chunks(go)

    rows_loop(0, R, taps0)
    tap_sums = taps_stage0()
    finish(sums)
    sums = stage1(0)
    stage4(1)
    finish(moving)

    def last(r):
        def go(a):
            for lanes in groups:
                s = wide(g1[r, pl.ds(a, ch), :, lanes])
                for t, v in taps(g0p, r, a, lanes, True):
                    s = s + v * kb[0, t, :, lanes]
                hid1[r, pl.ds(a, ch), :, lanes] = s.reshape(ch, T, 128).astype(BF16)

        chunks(go)
        rows = jnp.dot(unperm[...], hid1[r].reshape(M, C), preferred_element_type=F32).astype(BF16)
        raw[pl.ds(S * r, S)] = rows.reshape(S, S * A, C)

    out_copies = []
    tap_stages = (taps_stage1, taps_stage2, taps_stage3)
    for i, stage in enumerate((stage2, stage3, None)):
        rows_loop(cuts[i], cuts[i + 1], last)
        for r in range(cuts[i], cuts[i + 1]):
            c = pltpu.make_async_copy(raw.at[pl.ds(S * r, S)], out_hbm.at[0, pl.ds(S * r, S)], out_sem.at[r])
            c.start()
            out_copies.append(c)
        finish(sums)
        sums = stage(0) if stage else []
        finish(tap_sums)
        tap_sums = tap_stages[i]()
    stage4(0)
    finish(out_copies)


def body(inputs, cotangent, dw_kernel, pw_weight):
    _, rows, cols, C = inputs.shape
    n = lax.axis_size("lon")
    R, A, T, H = rows // S, cols // S, S * S, C // 2
    piece = H // n
    wire = BF16 if piece % 16 == 0 else F32
    samples = inputs.size // C * n * lax.axis_size("lat") * lax.axis_size("mem")
    anywhere = pl.BlockSpec(memory_space=pl.ANY)
    local = pl.BlockSpec(memory_space=pltpu.VMEM)
    padded = pltpu.VMEM((R + 2, A + 2, T, C), BF16)
    cells = pltpu.VMEM((R, A, T, C), BF16)
    scratch = [
        pltpu.VMEM((rows, cols, C), BF16),
        pltpu.VMEM((rows, cols, C), BF16),
        padded, padded, padded, padded,
        cells, cells, cells, cells,
        pltpu.VMEM((R, A, T, C), F32),
        pltpu.VMEM((R, A, T, 128), F32),
        pltpu.VMEM((1, A, T, 128), F32),
        pltpu.VMEM((A, T, C), F32),
        pltpu.VMEM((A * T, A * T), BF16),
        pltpu.VMEM((A * T, A * T), BF16),
        pltpu.VMEM((2, 9, 8, C), F32),
        pltpu.VMEM((2, 9, 8, C), F32),
        pltpu.VMEM((2, C, C), F32),
        pltpu.VMEM((2, H, C), BF16), pltpu.VMEM((2, H, C), BF16),
        pltpu.VMEM((2, H, H), BF16), pltpu.VMEM((2, H, H), BF16),
        pltpu.VMEM((2, n, piece, H), wire), pltpu.VMEM((2, n, piece, H), wire),
        pltpu.VMEM((2, piece, H), wire), pltpu.VMEM((2, 2, n, piece, H), wire),
        pltpu.VMEM((2, 16, C), F32), pltpu.VMEM((2, 16, C), F32),
        pltpu.VMEM((2, 16, H), F32), pltpu.VMEM((2, 16, H), F32),
        pltpu.VMEM((2, 16, H), BF16), pltpu.VMEM((n, 2, 16, H), BF16),
        pltpu.SemaphoreType.DMA((2, R)), pltpu.SemaphoreType.DMA((R,)),
        pltpu.SemaphoreType.DMA((4, 5)), pltpu.SemaphoreType.DMA((4, 5)),
        pltpu.SemaphoreType.DMA((2, 4, 2 * n)), pltpu.SemaphoreType.DMA((2, 4, 2 * n)),
    ]
    return pl.pallas_call(
        functools.partial(kernel, n, 1.0 / math.sqrt(samples)),
        out_shape=(
            jax.ShapeDtypeStruct(inputs.shape, BF16),
            jax.ShapeDtypeStruct((2, 9, H), F32),
            jax.ShapeDtypeStruct((2, C, H), F32),
        ),
        in_specs=[anywhere, anywhere, local, local],
        out_specs=(anywhere, local, local),
        scratch_shapes=scratch,
        name="blocks",
        compiler_params=pltpu.CompilerParams(
            collective_id=0, has_side_effects=True, vmem_limit_bytes=60 * 1024 * 1024
        ),
    )(inputs, cotangent, dw_kernel, pw_weight)


def solution(mesh):
    placed = (P("mem", "lat", "lon", None), P("mem", "lat", "lon", None), P(), P())
    return jax.shard_map(
        body,
        mesh=mesh,
        in_specs=placed,
        out_specs=(P("mem", "lat", "lon", None), P(None, None, "mem"), P(None, None, "mem")),
        check_vma=False,
    )
```
